256 devices in a mesh: section: 16 (over z, core), tensor: 16 (over y, x).
Axes of the slice: x: 4, y: 4, z: 8, core: 2. Of those that a mesh axis runs over, the one named last changes fastest.
Arguments:
- stream: float32 [16, 512, 8192], P('section', None, 'tensor'), may hold values from -40 to 40
- down_factor: bfloat16 [2, 16, 8192, 512], P(None, 'section', 'tensor'), may hold values from -0.0625 to 0.0625
- router: bfloat16 [2, 16, 8192, 512], P(None, 'section', 'tensor'), may hold values from -0.0625 to 0.0625
- expert_factor: bfloat16 [2, 16, 512, 32], P(None, 'section'), may hold values from -0.25 to 0.25
- core_tensor: bfloat16 [2, 16, 512, 32, 512], P(None, 'section', 'tensor'), may hold values from -0.046875 to 0.046875
- up_factor: bfloat16 [2, 16, 512, 8192], P(None, 'section', None, 'tensor'), may hold values from -0.25 to 0.25
Outputs:
- stream_out: float32 [16, 512, 8192], P('section', None, 'tensor')
The draws below stay inside these ranges and needn't reach their ends.
All inputs are finite; a program needn't handle non-finite values.
Results may differ from the reference program's by a relative error of at most 0.0095.
Values may be sent and summed in bfloat16 or wider, within the bound.
A program may use at most 64 MiB of HBM per device.

```python
import math
import jax
import jax.numpy as jnp
from jax import lax

D = 8192
EXPERTS = 512
RE = 32
RD = 512
RF = 512
LAPS = 2
TICKS = 6
MB = 512
SECTIONS = 16
FRONT = 8


def draw_stream(key, part):
    subkeys = jax.random.split(key, 3)
    positions = jnp.arange(D, dtype=jnp.float32) / D
    entries = jax.random.normal(subkeys[0], (SECTIONS, MB, D), jnp.float32)
    ramp_up = 1.0 + 5.0 * positions
    row_scale = jnp.exp(jax.random.uniform(subkeys[2], (SECTIONS, MB, 1), jnp.float32, math.log(0.3), math.log(3.0)))
    col_scale = jnp.exp(jax.random.uniform(subkeys[1], (D,), jnp.float32, 0.0, math.log(10.0))) * jnp.sqrt(ramp_up) / 8.0
    return jnp.clip(entries * col_scale * row_scale, -40.0, 40.0).astype(jnp.float32)


def level_of(key, shape, shards, least, high):
    level, own = 1.0, jax.random.fold_in(key, 6)
    for axis_at, blocks in shards:
        heights = jnp.exp(jax.random.uniform(jax.random.fold_in(own, axis_at), (blocks,), jnp.float32, least / len(shards), high / len(shards)))
        level = level * jnp.repeat(heights, shape[axis_at] // blocks).reshape([-1 if axis == axis_at else 1 for axis in range(len(shape))])
    return level


def scatter_about(key, extent, width, limit, cuts=(), kind=jnp.bfloat16):
    values = width * jax.random.normal(key, extent, jnp.float32)
    if cuts:
        values = values * level_of(key, extent, cuts, -0.22, 0.18)
    return jnp.clip(values, -limit, limit).astype(kind)


def setup_inputs(seed: int = 0) -> dict:
    splits = jax.random.split(jax.random.key(seed), 7)
    stream = draw_stream(jax.random.fold_in(splits[6], 71), 0)
    down_factor = scatter_about(splits[1], (LAPS, SECTIONS, D, RD), D ** -0.5, 0.0625, ((1, 16), (2, 16)))
    router = scatter_about(splits[2], (LAPS, SECTIONS, D, EXPERTS), D ** -0.5, 0.0625, ((1, 16), (2, 16)))
    expert_factor = scatter_about(splits[3], (LAPS, SECTIONS, EXPERTS, RE), EXPERTS ** -0.5, 0.25, ((1, 16),))
    core_tensor = scatter_about(splits[4], (LAPS, SECTIONS, RF, RE, RD), (RE * RD) ** -0.5, 0.046875, ((1, 16), (2, 16)))
    up_factor = scatter_about(splits[5], (LAPS, SECTIONS, RF, D), RF ** -0.5, 0.25, ((1, 16), (3, 16)))
    return {"stream": stream, "down_factor": down_factor, "router": router, "expert_factor": expert_factor, "core_tensor": core_tensor, "up_factor": up_factor}


EPSILON = 1e-05

def section_layer(current, down_part, router_part, expert_part, core_part, up_part):
    lowered = current.astype(jnp.bfloat16)
    projected = jnp.dot(lowered, down_part, preferred_element_type=jnp.float32)
    logits = jnp.dot(lowered, router_part, preferred_element_type=jnp.float32)
    factor = lax.rsqrt(lax.optimization_barrier(jnp.sum(current * current, axis=1, keepdims=True)) / D + EPSILON)
    reduced = (projected * factor).astype(jnp.bfloat16)
    gating = jax.nn.sigmoid(logits * factor).astype(jnp.bfloat16)
    mixing = jnp.dot(gating, expert_part, preferred_element_type=jnp.float32).astype(jnp.bfloat16)
    flattened = core_part.reshape(RF * RE, RD)
    partial_value = lax.dot_general(reduced, flattened, (((1,), (1,)), ((), ())), preferred_element_type=jnp.float32)
    partial_value = partial_value.reshape(MB, RF, RE)
    ranked = lax.optimization_barrier(jnp.sum(partial_value * mixing.astype(jnp.float32)[:, None, :], axis=2)).astype(jnp.bfloat16)
    return current + jnp.dot(ranked, up_part, preferred_element_type=jnp.float32)

def reference(stream, down_factor, router, expert_factor, core_tensor, up_factor):
    section_ids = jnp.arange(SECTIONS, dtype=jnp.int32)
    carried = stream
    for tick_index in range(TICKS):
        anchor = (section_ids - tick_index) % SECTIONS
        lap_ids = (anchor < FRONT).astype(jnp.int32) + (section_ids < tick_index).astype(jnp.int32)

        def one_section(section_inputs):
            current, lap_id, section_id = section_inputs
            return section_layer(current, down_factor[lap_id, section_id], router[lap_id, section_id], expert_factor[lap_id, section_id], core_tensor[lap_id, section_id], up_factor[lap_id, section_id])
        advanced = lax.map(one_section, (carried, lap_ids, section_ids))
        carried = jnp.roll(advanced, 1, axis=0)
    return carried
```

```python
import functools

import jax
import jax.numpy as jnp
from jax import lax
from jax.experimental import pallas as pl
from jax.experimental.pallas import tpu as pltpu
from jax.sharding import PartitionSpec as P

D = 8192
TICKS = 6
EPSILON = 1e-05
MB = 512
RANK = 512
EX = 32
FB = 32
NT = 16
C = 2
T = MB // C
TB = T // NT
G = TB // 8
MESH = pl.DeviceIdType.MESH
F32 = jnp.float32
BF16 = jnp.bfloat16
NT_DIMS = (((1,), (1,)), ((), ()))
TN_DIMS = (((0,), (0,)), ((), ()))


def kernel(
    stream, down, router, expert, core, up, out,
    w_down, w_router, w_expert, w_core, w_up, expert4, selector, unpack, ones,
    h, square_own, square_in, logit_own, logit_in, proj_own, proj_in, reduced, mixing, ranked,
    load_sem, h_send, h_recv, square_send, square_recv, logit_send, logit_recv,
    proj_send, proj_recv, reduced_send, reduced_recv, mixing_send, mixing_recv, ranked_send, ranked_recv, out_sem,
):
    me = lax.axis_index("tensor")
    section = lax.axis_index("section")
    sections = lax.axis_size("section")
    after = lax.rem(section + 1, sections)
    before = lax.rem(section + sections - 1, sections)

    loads = []
    for c in range(C):
        loads.append(pltpu.make_async_copy(stream.at[0, pl.ds(c * T, T)], h.at[0, c], load_sem.at[c]))
    for i, (a, b) in enumerate(
        ((router, w_router), (down, w_down), (expert, w_expert), (core, w_core), (up, w_up))
    ):
        loads.append(pltpu.make_async_copy(a, b, load_sem.at[C + i]))
    for copy in loads:
        copy.start()

    barrier = pltpu.get_barrier_semaphore()
    for d in range(1, NT):
        pl.semaphore_signal(barrier, inc=1, device_id={"tensor": lax.rem(me + d, NT)}, device_id_type=MESH)
    pl.semaphore_signal(barrier, inc=1, device_id={"section": after}, device_id_type=MESH)
    pl.semaphore_signal(barrier, inc=1, device_id={"section": before}, device_id_type=MESH)

    ones[...] = jnp.ones((8, MB), BF16)
    rows = lax.broadcasted_iota(jnp.int32, (FB, FB * EX), 0)
    columns = lax.broadcasted_iota(jnp.int32, (FB, FB * EX), 1)
    selector[...] = jnp.where(columns // EX == rows, 1.0, 0.0).astype(BF16)
    rows = lax.broadcasted_iota(jnp.int32, (128, 128), 0)
    columns = lax.broadcasted_iota(jnp.int32, (128, 128), 1)
    for g in range(G):
        unpack[g] = jnp.where(rows == g * EX + columns % EX, 1.0, 0.0).astype(BF16)

    for copy in loads:
        copy.wait()
    for lap in range(2):
        one = w_expert[lap, 0]
        expert4[lap] = jnp.concatenate([one, one, one, one], axis=1)

    pl.semaphore_wait(barrier, NT + 1)

    def to_peers(source, target, send, recv):
        for d in range(1, NT):
            peer = lax.rem(me + d, NT)
            pltpu.make_async_remote_copy(
                source(d, peer), target(d), send, recv, device_id={"tensor": peer}, device_id_type=MESH
            ).start()

    def wait_bytes(ref, sem):
        pltpu.make_async_copy(ref, ref, sem).wait()

    def project(k, c, lap):
        x = h[k, c]

        @pl.when(k > 0)
        def _():
            wait_bytes(square_in.at[0, c], square_send.at[c])
            wait_bytes(logit_own.at[c, pl.ds(0, NT - 1)], logit_send.at[c])
            wait_bytes(proj_own.at[c, pl.ds(0, NT - 1)], proj_send.at[c])

        squares = lax.dot_general(ones[...], (x * x).astype(BF16), NT_DIMS, preferred_element_type=F32)
        square_own[c] = squares[0:1]
        to_peers(lambda d, p: square_own.at[c], lambda d: square_in.at[k, c, d - 1], square_send.at[c], square_recv.at[k, c])
        low = x.astype(BF16)
        part = jnp.dot(low, w_router[lap, 0], preferred_element_type=F32)
        logit_own[c] = part.astype(BF16).reshape(NT, TB, RANK)
        to_peers(lambda d, p: logit_own.at[c, p], lambda d: logit_in.at[k, c, d - 1], logit_send.at[c], logit_recv.at[k, c])
        part = jnp.dot(low, w_down[lap, 0], preferred_element_type=F32)
        proj_own[c] = part.astype(BF16).reshape(NT, TB, RANK)
        to_peers(lambda d, p: proj_own.at[c, p], lambda d: proj_in.at[k, c, d - 1], proj_send.at[c], proj_recv.at[k, c])

    def finish(k, c, lap):
        wait_bytes(square_in.at[k, c], square_recv.at[k, c])
        total = square_own[c]
        for d in range(NT - 1):
            total = total + square_in[k, c, d]
        at = lax.broadcasted_iota(jnp.int32, (TB, T), 1) == me * TB + lax.broadcasted_iota(jnp.int32, (TB, T), 0)
        own = jnp.sum(jnp.where(at, jnp.broadcast_to(total, (TB, T)), 0.0), axis=1, keepdims=True)
        factor = lax.rsqrt(own / D + EPSILON)

        wait_bytes(logit_in.at[k, c], logit_recv.at[k, c])
        logits = logit_own[c, me].astype(F32)
        for d in range(NT - 1):
            logits = logits + logit_in[k, c, d].astype(F32)
        gating = jax.nn.sigmoid(logits * factor).astype(BF16)
        mixed = jnp.dot(gating, expert4[lap], preferred_element_type=F32)
        mixed = mixed.astype(BF16).astype(F32)
        lane = lax.broadcasted_iota(jnp.int32, (8, 128), 1) // EX
        packed = jnp.zeros((8, 128), F32)
        for g in range(G):
            packed = jnp.where(lane == g, mixed[g * 8 : g * 8 + 8], packed)
        mixing[k, c, me] = packed
        to_peers(lambda d, p: mixing.at[k, c, me], lambda d: mixing.at[k, c, me], mixing_send.at[c], mixing_recv.at[k, c])

        wait_bytes(proj_in.at[k, c], proj_recv.at[k, c])
        projected = proj_own[c, me].astype(F32)
        for d in range(NT - 1):
            projected = projected + proj_in[k, c, d].astype(F32)
        reduced[k, c, me] = (projected * factor).astype(BF16)
        to_peers(lambda d, p: reduced.at[k, c, me], lambda d: reduced.at[k, c, me], reduced_send.at[c], reduced_recv.at[k, c])

    def core_stage(k, c, lap):
        wait_bytes(mixing.at[k, c, pl.ds(0, NT - 1)], mixing_recv.at[k, c])
        packed = mixing[k, c].reshape(128, 128).astype(BF16)
        wait_bytes(reduced.at[k, c, pl.ds(0, NT - 1)], reduced_recv.at[k, c])
        part = lax.dot_general(
            reduced[k, c].reshape(T, RANK), w_core[lap, 0].reshape(FB * EX, RANK), NT_DIMS, preferred_element_type=F32
        ).reshape(NT, G, 8, FB * EX)
        for g in range(G):
            weights = jnp.dot(packed, unpack[g], preferred_element_type=F32).reshape(NT, 8, 128)
            weights = jnp.concatenate([weights] * (FB * EX // 128), axis=2)
            product = (part[:, g] * weights).reshape(128, FB * EX).astype(BF16)
            ranked[k, c, me, :, g * 128 : g * 128 + 128] = lax.dot_general(
                selector[...], product, NT_DIMS, preferred_element_type=F32
            ).astype(BF16)
        to_peers(lambda d, p: ranked.at[k, c, me], lambda d: ranked.at[k, c, me], ranked_send.at[c], ranked_recv.at[k, c])

    def advance(k, c, lap):
        wait_bytes(ranked.at[k, c, pl.ds(0, NT - 1)], ranked_recv.at[k, c])
        update = lax.dot_general(
            ranked[k, c].reshape(RANK, T), w_up[lap, 0], TN_DIMS, preferred_element_type=F32
        )
        update = update.reshape(G, NT, 8, 512)
        for g in range(G):
            rows = h[k, c].reshape(NT, G, 8, 512)[:, g] + update[g]
            for j in range(NT):
                h[k, c, (j * G + g) * 8 : (j * G + g) * 8 + 8] = rows[j]
        pltpu.make_async_remote_copy(
            h.at[k, c], h.at[k + 1, c], h_send.at[c], h_recv.at[k + 1, c],
            device_id={"section": after}, device_id_type=MESH,
        ).start()

    def tick(k, carry):
        anchor = lax.rem(section - k + sections, sections)
        lap = jnp.where(anchor < sections // 2, 1, 0) + jnp.where(section < k, 1, 0)
        for c in range(C):

            @pl.when(k > 0)
            def _():
                wait_bytes(h.at[k, c], h_recv.at[k, c])

            project(k, c, lap)
        for c in range(C):
            finish(k, c, lap)
        for c in range(C):
            core_stage(k, c, lap)
        for c in range(C):
            advance(k, c, lap)
        return carry

    lax.fori_loop(0, TICKS, tick, 0)
    copies = []
    for c in range(C):
        wait_bytes(h.at[TICKS, c], h_recv.at[TICKS, c])
        copies.append(pltpu.make_async_copy(h.at[TICKS, c], out.at[0, pl.ds(c * T, T)], out_sem.at[c]))
        copies[-1].start()
    for c in range(C):
        wait_bytes(square_in.at[0, c], square_send.at[c])
        wait_bytes(logit_own.at[c, pl.ds(0, NT - 1)], logit_send.at[c])
        wait_bytes(proj_own.at[c, pl.ds(0, NT - 1)], proj_send.at[c])
        wait_bytes(mixing.at[:, c, pl.ds(0, NT - 1)], mixing_send.at[c])
        wait_bytes(reduced.at[:, c, pl.ds(0, NT - 1)], reduced_send.at[c])
        wait_bytes(ranked.at[:, c, pl.ds(0, NT - 1)], ranked_send.at[c])
        wait_bytes(h.at[pl.ds(0, TICKS), c], h_send.at[c])
    for copy in copies:
        copy.wait()


def per_device(stream, down_factor, router, expert_factor, core_tensor, up_factor):
    operands = (stream, down_factor, router, expert_factor, core_tensor, up_factor)
    dma = pltpu.SemaphoreType.DMA
    return pl.pallas_call(
        kernel,
        out_shape=jax.ShapeDtypeStruct(stream.shape, F32),
        in_specs=[pl.BlockSpec(memory_space=pl.ANY)] * len(operands),
        out_specs=pl.BlockSpec(memory_space=pl.ANY),
        scratch_shapes=[
            pltpu.VMEM(down_factor.shape, BF16),
            pltpu.VMEM(router.shape, BF16),
            pltpu.VMEM(expert_factor.shape, BF16),
            pltpu.VMEM(core_tensor.shape, BF16),
            pltpu.VMEM(up_factor.shape, BF16),
            pltpu.VMEM((2, RANK, 128), BF16),
            pltpu.VMEM((FB, FB * EX), BF16),
            pltpu.VMEM((G, 128, 128), BF16),
            pltpu.VMEM((8, MB), BF16),
            pltpu.VMEM((TICKS + 1, C, T, 512), F32),
            pltpu.VMEM((C, 1, T), F32),
            pltpu.VMEM((TICKS, C, NT - 1, 1, T), F32),
            pltpu.VMEM((C, NT, TB, RANK), BF16),
            pltpu.VMEM((TICKS, C, NT - 1, TB, RANK), BF16),
            pltpu.VMEM((C, NT, TB, RANK), BF16),
            pltpu.VMEM((TICKS, C, NT - 1, TB, RANK), BF16),
            pltpu.VMEM((TICKS, C, NT, TB, RANK), BF16),
            pltpu.VMEM((TICKS, C, NT, 8, 128), F32),
            pltpu.VMEM((TICKS, C, NT, FB, T), BF16),
            dma((C + 5,)),
            dma((C,)),
            dma((TICKS + 1, C)),
            dma((C,)),
            dma((TICKS, C)),
            dma((C,)),
            dma((TICKS, C)),
            dma((C,)),
            dma((TICKS, C)),
            dma((C,)),
            dma((TICKS, C)),
            dma((C,)),
            dma((TICKS, C)),
            dma((C,)),
            dma((TICKS, C)),
            dma((C,)),
        ],
        compiler_params=pltpu.CompilerParams(
            collective_id=0, has_side_effects=True, vmem_limit_bytes=60 << 20
        ),
        name="relay_window",
    )(*operands)


def solution(mesh):
    return jax.shard_map(
        per_device,
        mesh=mesh,
        in_specs=(
            P("section", None, "tensor"),
            P(None, "section", "tensor", None),
            P(None, "section", "tensor", None),
            P(None, "section", None, None),
            P(None, "section", "tensor", None, None),
            P(None, "section", None, "tensor"),
        ),
        out_specs=P("section", None, "tensor"),
        check_vma=False,
    )
```

```python
import functools

import jax
import jax.numpy as jnp
from jax import lax
from jax.experimental import pallas as pl
from jax.experimental.pallas import tpu as pltpu
from jax.sharding import PartitionSpec as P

D = 8192
TICKS = 6
EPSILON = 1e-05
MB = 512
RANK = 512
EX = 32
FB = 32
NT = 16
C = 2
T = MB // C
TB = T // NT
G = TB // 8
MESH = pl.DeviceIdType.MESH
F32 = jnp.float32
BF16 = jnp.bfloat16
NT_DIMS = (((1,), (1,)), ((), ()))
TN_DIMS = (((0,), (0,)), ((), ()))


def kernel(
    stream, down, router, expert, core, up, out,
    w_down, w_router, w_expert, w_core, up_in, expert4, selector, unpack, ones,
    h, square_own, square_in, logit_own, logit_in, proj_own, proj_in, reduced, mixing, ranked_own, ranked,
    load_sem, up_send, up_recv, h_send, h_recv, square_send, square_recv, logit_send, logit_recv,
    proj_send, proj_recv, reduced_send, reduced_recv, mixing_send, mixing_recv, ranked_send, ranked_recv, out_sem,
):
    me = lax.axis_index("tensor")
    section = lax.axis_index("section")
    sections = lax.axis_size("section")
    after = lax.rem(section + 1, sections)
    before = lax.rem(section + sections - 1, sections)

    loads = []
    for c in range(C):
        loads.append(pltpu.make_async_copy(stream.at[0, pl.ds(c * T, T)], h.at[0, c], load_sem.at[c]))
    for i, (a, b) in enumerate(
        ((router, w_router), (down, w_down), (expert, w_expert), (core, w_core))
    ):
        loads.append(pltpu.make_async_copy(a, b, load_sem.at[C + i]))
    for copy in loads:
        copy.start()

    barrier = pltpu.get_barrier_semaphore()
    for d in range(NT):
        peer = lax.rem(me + d, NT)
        if d:
            pl.semaphore_signal(barrier, inc=1, device_id={"tensor": peer}, device_id_type=MESH)
        pl.semaphore_signal(barrier, inc=1, device_id={"section": before, "tensor": peer}, device_id_type=MESH)

    ones[...] = jnp.ones((8, MB), BF16)
    rows = lax.broadcasted_iota(jnp.int32, (FB, FB * EX), 0)
    columns = lax.broadcasted_iota(jnp.int32, (FB, FB * EX), 1)
    selector[...] = jnp.where(columns // EX == rows, 1.0, 0.0).astype(BF16)
    rows = lax.broadcasted_iota(jnp.int32, (128, 128), 0)
    columns = lax.broadcasted_iota(jnp.int32, (128, 128), 1)
    for g in range(G):
        unpack[g] = jnp.where(rows == g * EX + columns % EX, 1.0, 0.0).astype(BF16)

    for copy in loads:
        copy.wait()
    for lap in range(2):
        one = w_expert[lap, 0]
        expert4[lap] = jnp.concatenate([one, one, one, one], axis=1)

    pl.semaphore_wait(barrier, 2 * NT - 1)

    def lap_of(s, k):
        return jnp.where(lax.rem(s - k + sections, sections) < sections // 2, 1, 0) + jnp.where(s < k, 1, 0)

    def hand_up(lap):
        pltpu.make_async_remote_copy(
            up.at[lap], up_in.at[lap], up_send.at[lap], up_recv.at[lap],
            device_id={"section": after}, device_id_type=MESH,
        ).start()

    hand_up(lap_of(section, 0))

    def to_peers(source, target, send, recv):
        for d in range(1, NT):
            peer = lax.rem(me + d, NT)
            pltpu.make_async_remote_copy(
                source(d, peer), target(d), send, recv, device_id={"tensor": peer}, device_id_type=MESH
            ).start()

    def wait_bytes(ref, sem):
        pltpu.make_async_copy(ref, ref, sem).wait()

    def project(k, c, lap):
        x = h[k, c]

        @pl.when(k > 0)
        def _():
            wait_bytes(square_in.at[0, c], square_send.at[c])
            wait_bytes(logit_own.at[c, pl.ds(0, NT - 1)], logit_send.at[c])
            wait_bytes(proj_own.at[c, pl.ds(0, NT - 1)], proj_send.at[c])

        squares = lax.dot_general(ones[...], (x * x).astype(BF16), NT_DIMS, preferred_element_type=F32)
        square_own[c] = squares[0:1]
        to_peers(lambda d, p: square_own.at[c], lambda d: square_in.at[k, c, d - 1], square_send.at[c], square_recv.at[k, c])
        low = x.astype(BF16)
        part = jnp.dot(low, w_router[lap, 0], preferred_element_type=F32)
        logit_own[c] = part.astype(BF16).reshape(NT, TB, RANK)
        to_peers(lambda d, p: logit_own.at[c, p], lambda d: logit_in.at[k, c, d - 1], logit_send.at[c], logit_recv.at[k, c])
        part = jnp.dot(low, w_down[lap, 0], preferred_element_type=F32)
        proj_own[c] = part.astype(BF16).reshape(NT, TB, RANK)
        to_peers(lambda d, p: proj_own.at[c, p], lambda d: proj_in.at[k, c, d - 1], proj_send.at[c], proj_recv.at[k, c])

    def finish(k, c, lap):
        wait_bytes(square_in.at[k, c], square_recv.at[k, c])
        total = square_own[c]
        for d in range(NT - 1):
            total = total + square_in[k, c, d]
        at = lax.broadcasted_iota(jnp.int32, (TB, T), 1) == me * TB + lax.broadcasted_iota(jnp.int32, (TB, T), 0)
        own = jnp.sum(jnp.where(at, jnp.broadcast_to(total, (TB, T)), 0.0), axis=1, keepdims=True)
        factor = lax.rsqrt(own / D + EPSILON)

        wait_bytes(logit_in.at[k, c], logit_recv.at[k, c])
        logits = logit_own[c, me].astype(F32)
        for d in range(NT - 1):
            logits = logits + logit_in[k, c, d].astype(F32)
        gating = jax.nn.sigmoid(logits * factor).astype(BF16)
        mixed = jnp.dot(gating, expert4[lap], preferred_element_type=F32)
        mixed = mixed.astype(BF16).astype(F32)
        lane = lax.broadcasted_iota(jnp.int32, (8, 128), 1) // EX
        packed = jnp.zeros((8, 128), F32)
        for g in range(G):
            packed = jnp.where(lane == g, mixed[g * 8 : g * 8 + 8], packed)
        mixing[k, c, me] = packed
        to_peers(lambda d, p: mixing.at[k, c, me], lambda d: mixing.at[k, c, me], mixing_send.at[c], mixing_recv.at[k, c])

        wait_bytes(proj_in.at[k, c], proj_recv.at[k, c])
        projected = proj_own[c, me].astype(F32)
        for d in range(NT - 1):
            projected = projected + proj_in[k, c, d].astype(F32)
        reduced[k, c, me] = (projected * factor).astype(BF16)
        to_peers(lambda d, p: reduced.at[k, c, me], lambda d: reduced.at[k, c, me], reduced_send.at[c], reduced_recv.at[k, c])

    def core_stage(k, c, lap):
        wait_bytes(mixing.at[k, c, pl.ds(0, NT - 1)], mixing_recv.at[k, c])
        packed = mixing[k, c].reshape(128, 128).astype(BF16)
        wait_bytes(reduced.at[k, c, pl.ds(0, NT - 1)], reduced_recv.at[k, c])
        part = lax.dot_general(
            reduced[k, c].reshape(T, RANK), w_core[lap, 0].reshape(FB * EX, RANK), NT_DIMS, preferred_element_type=F32
        ).reshape(NT, G, 8, FB * EX)
        for g in range(G):
            weights = jnp.dot(packed, unpack[g], preferred_element_type=F32).reshape(NT, 8, 128)
            weights = jnp.concatenate([weights] * (FB * EX // 128), axis=2)
            product = (part[:, g] * weights).reshape(128, FB * EX).astype(BF16)
            ranked_own[k, c, :, g * 128 : g * 128 + 128] = lax.dot_general(
                selector[...], product, NT_DIMS, preferred_element_type=F32
            ).astype(BF16)
        for d in range(NT):
            pltpu.make_async_remote_copy(
                ranked_own.at[k, c], ranked.at[k, c, me], ranked_send.at[c], ranked_recv.at[k, c],
                device_id={"section": after, "tensor": lax.rem(me + d, NT)}, device_id_type=MESH,
            ).start()

    def advance(k, c, lap):
        wait_bytes(h.at[k + 1, c], h_recv.at[k + 1, c])
        wait_bytes(ranked.at[k, c], ranked_recv.at[k, c])
        update = lax.dot_general(
            ranked[k, c].reshape(RANK, T), up_in[lap, 0], TN_DIMS, preferred_element_type=F32
        )
        update = update.reshape(G, NT, 8, 512)
        for g in range(G):
            rows = h[k + 1, c].reshape(NT, G, 8, 512)[:, g] + update[g]
            for j in range(NT):
                h[k + 1, c, (j * G + g) * 8 : (j * G + g) * 8 + 8] = rows[j]

    def hand_on(k, c):
        pltpu.make_async_remote_copy(
            h.at[k, c], h.at[k + 1, c], h_send.at[c], h_recv.at[k + 1, c],
            device_id={"section": after}, device_id_type=MESH,
        ).start()

    def tick(k, carry):
        lap = lap_of(section, k)
        earlier = lap_of(before, k - 1)
        for c in range(C):

            @pl.when(k > 0)
            def _():
                if c == 0:

                    @pl.when(k < 3)
                    def _():
                        which = jnp.where(k == 1, lap_of(before, 0), 1 - lap_of(before, 0))
                        wait_bytes(up_in.at[which], up_recv.at[which])

                advance(k - 1, c, earlier)

            hand_on(k, c)
            project(k, c, lap)

        @pl.when(k == 1)
        def _():
            hand_up(1 - lap_of(section, 0))

        for c in range(C):
            finish(k, c, lap)
        for c in range(C):
            core_stage(k, c, lap)
        return carry

    lax.fori_loop(0, TICKS, tick, 0)
    copies = []
    for c in range(C):
        advance(TICKS - 1, c, lap_of(before, TICKS - 1))
        copies.append(pltpu.make_async_copy(h.at[TICKS, c], out.at[0, pl.ds(c * T, T)], out_sem.at[c]))
        copies[-1].start()
    for c in range(C):
        wait_bytes(square_in.at[0, c], square_send.at[c])
        wait_bytes(logit_own.at[c, pl.ds(0, NT - 1)], logit_send.at[c])
        wait_bytes(proj_own.at[c, pl.ds(0, NT - 1)], proj_send.at[c])
        wait_bytes(mixing.at[:, c, pl.ds(0, NT - 1)], mixing_send.at[c])
        wait_bytes(reduced.at[:, c, pl.ds(0, NT - 1)], reduced_send.at[c])
        wait_bytes(ranked.at[:, c], ranked_send.at[c])
        wait_bytes(h.at[pl.ds(0, TICKS), c], h_send.at[c])
    for lap in range(2):
        wait_bytes(up_in.at[lap], up_send.at[lap])
    for copy in copies:
        copy.wait()


def per_device(stream, down_factor, router, expert_factor, core_tensor, up_factor):
    operands = (stream, down_factor, router, expert_factor, core_tensor, up_factor)
    dma = pltpu.SemaphoreType.DMA
    return pl.pallas_call(
        kernel,
        out_shape=jax.ShapeDtypeStruct(stream.shape, F32),
        in_specs=[pl.BlockSpec(memory_space=pl.ANY)] * len(operands),
        out_specs=pl.BlockSpec(memory_space=pl.ANY),
        scratch_shapes=[
            pltpu.VMEM(down_factor.shape, BF16),
            pltpu.VMEM(router.shape, BF16),
            pltpu.VMEM(expert_factor.shape, BF16),
            pltpu.VMEM(core_tensor.shape, BF16),
            pltpu.VMEM(up_factor.shape, BF16),
            pltpu.VMEM((2, RANK, 128), BF16),
            pltpu.VMEM((FB, FB * EX), BF16),
            pltpu.VMEM((G, 128, 128), BF16),
            pltpu.VMEM((8, MB), BF16),
            pltpu.VMEM((TICKS + 1, C, T, 512), F32),
            pltpu.VMEM((C, 1, T), F32),
            pltpu.VMEM((TICKS, C, NT - 1, 1, T), F32),
            pltpu.VMEM((C, NT, TB, RANK), BF16),
            pltpu.VMEM((TICKS, C, NT - 1, TB, RANK), BF16),
            pltpu.VMEM((C, NT, TB, RANK), BF16),
            pltpu.VMEM((TICKS, C, NT - 1, TB, RANK), BF16),
            pltpu.VMEM((TICKS, C, NT, TB, RANK), BF16),
            pltpu.VMEM((TICKS, C, NT, 8, 128), F32),
            pltpu.VMEM((TICKS, C, FB, T), BF16),
            pltpu.VMEM((TICKS, C, NT, FB, T), BF16),
            dma((C + 4,)),
            dma((2,)),
            dma((2,)),
            dma((C,)),
            dma((TICKS + 1, C)),
            dma((C,)),
            dma((TICKS, C)),
            dma((C,)),
            dma((TICKS, C)),
            dma((C,)),
            dma((TICKS, C)),
            dma((C,)),
            dma((TICKS, C)),
            dma((C,)),
            dma((TICKS, C)),
            dma((C,)),
            dma((TICKS, C)),
            dma((C,)),
        ],
        compiler_params=pltpu.CompilerParams(
            collective_id=0, has_side_effects=True, vmem_limit_bytes=60 << 20
        ),
        name="relay_window",
    )(*operands)


def solution(mesh):
    return jax.shard_map(
        per_device,
        mesh=mesh,
        in_specs=(
            P("section", None, "tensor"),
            P(None, "section", "tensor", None),
            P(None, "section", "tensor", None),
            P(None, "section", None, None),
            P(None, "section", "tensor", None, None),
            P(None, "section", None, "tensor"),
        ),
        out_specs=P("section", None, "tensor"),
        check_vma=False,
    )
```

```python
import functools

import jax
import jax.numpy as jnp
from jax import lax
from jax.experimental import pallas as pl
from jax.experimental.pallas import tpu as pltpu
from jax.sharding import PartitionSpec as P

D = 8192
TICKS = 6
EPSILON = 1e-05
MB = 512
RANK = 512
EX = 32
FB = 32
NT = 16
C = 4
T = MB // C
TB = T // NT
RP = TB // 4
MESH = pl.DeviceIdType.MESH
F32 = jnp.float32
BF16 = jnp.bfloat16
NT_DIMS = (((1,), (1,)), ((), ()))
TN_DIMS = (((0,), (0,)), ((), ()))


def kernel(
    stream, down, router, expert, core, up, out,
    w_down, w_router, w_expert, w_core, up_in, expert4, selector, spread, group, tile4, ones,
    h, square_own, square_mid, square_sum, square_in, logit_own, logit_mid, logit_sum, logit_in,
    proj_own, proj_mid, proj_sum, proj_in, reduced, mixing, ranked_own, ranked,
    load_sem, up_send, up_recv, h_send, h_recv, first_send, first_recv, second_send, second_recv, reduced_send, reduced_recv, mixing_send, mixing_recv, ranked_send, ranked_recv, out_sem,
):
    me = lax.axis_index("tensor")
    section = lax.axis_index("section")
    my_y, my_x = me // 4, lax.rem(me, 4)
    sections = lax.axis_size("section")
    after = lax.rem(section + 1, sections)
    before = lax.rem(section + sections - 1, sections)

    loads = []
    for c in range(C):
        loads.append(pltpu.make_async_copy(stream.at[0, pl.ds(c * T, T)], h.at[0, c], load_sem.at[c]))
    for i, (a, b) in enumerate(
        ((router, w_router), (down, w_down), (expert, w_expert), (core, w_core))
    ):
        loads.append(pltpu.make_async_copy(a, b, load_sem.at[C + i]))
    for copy in loads:
        copy.start()

    barrier = pltpu.get_barrier_semaphore()
    for d in range(NT):
        peer = lax.rem(me + d, NT)
        if d:
            pl.semaphore_signal(barrier, inc=1, device_id={"tensor": peer}, device_id_type=MESH)
        pl.semaphore_signal(barrier, inc=1, device_id={"section": before, "tensor": peer}, device_id_type=MESH)

    ones[...] = jnp.ones((8, MB), BF16)
    rows = lax.broadcasted_iota(jnp.int32, (FB, FB * EX), 0)
    columns = lax.broadcasted_iota(jnp.int32, (FB, FB * EX), 1)
    selector[...] = jnp.where(columns // EX == rows, 1.0, 0.0).astype(BF16)
    rows = lax.broadcasted_iota(jnp.int32, (128, 128), 0)
    columns = lax.broadcasted_iota(jnp.int32, (128, 128), 1)
    tile4[...] = jnp.where(rows % EX == columns % EX, 1.0, 0.0).astype(BF16)
    rows = lax.broadcasted_iota(jnp.int32, (T, NT * RP), 0)
    columns = lax.broadcasted_iota(jnp.int32, (T, NT * RP), 1)
    spread[...] = jnp.where((rows // TB == columns // RP) & (rows % RP == columns % RP), 1.0, 0.0).astype(BF16)
    rows = lax.broadcasted_iota(jnp.int32, (T, 128), 0)
    columns = lax.broadcasted_iota(jnp.int32, (T, 128), 1)
    group[...] = jnp.where((rows % TB) // RP == columns // EX, 1.0, 0.0)

    for copy in loads:
        copy.wait()
    for lap in range(2):
        one = w_expert[lap, 0]
        expert4[lap] = jnp.concatenate([one, one, one, one], axis=1)

    pl.semaphore_wait(barrier, 2 * NT - 1)

    def lap_of(s, k):
        return jnp.where(lax.rem(s - k + sections, sections) < sections // 2, 1, 0) + jnp.where(s < k, 1, 0)

    def hand_up(lap):
        pltpu.make_async_remote_copy(
            up.at[lap], up_in.at[lap], up_send.at[lap], up_recv.at[lap],
            device_id={"section": after}, device_id_type=MESH,
        ).start()

    hand_up(lap_of(section, 0))

    def to_peers(source, target, send, recv):
        for d in range(1, NT):
            peer = lax.rem(me + d, NT)
            pltpu.make_async_remote_copy(
                source(d, peer), target(d), send, recv, device_id={"tensor": peer}, device_id_type=MESH
            ).start()

    def along(axis, source, target, send, recv):
        for d in range(1, 4):
            if axis == "x":
                place = lax.rem(my_x + d, 4)
                peer = my_y * 4 + place
            else:
                place = lax.rem(my_y + d, 4)
                peer = place * 4 + my_x
            pltpu.make_async_remote_copy(
                source(place), target(d - 1), send, recv, device_id={"tensor": peer}, device_id_type=MESH
            ).start()

    def wait_bytes(ref, sem):
        pltpu.make_async_copy(ref, ref, sem).wait()

    def sums_sent(c):
        wait_bytes(square_mid.at[0, c], first_send.at[0, c])
        wait_bytes(logit_mid.at[0, c], first_send.at[1, c])
        wait_bytes(proj_mid.at[0, c], first_send.at[2, c])
        wait_bytes(square_in.at[0, c], second_send.at[0, c])
        wait_bytes(logit_in.at[0, c], second_send.at[1, c])
        wait_bytes(proj_in.at[0, c], second_send.at[2, c])

    def project(k, c, lap):
        x = h[k, c]

        @pl.when(k > 0)
        def _():
            sums_sent(c)

        squares = lax.dot_general(ones[...], (x * x).astype(BF16), NT_DIMS, preferred_element_type=F32)
        square_own[c] = squares[0:1]
        along("x", lambda p: square_own.at[c], lambda d: square_mid.at[k, c, d], first_send.at[0, c], first_recv.at[0, k, c])
        low = x.astype(BF16)
        part = jnp.dot(low, w_router[lap, 0], preferred_element_type=F32).reshape(4, 4, TB, RANK)
        for i in range(4):
            logit_own[c, i] = part[:, i].astype(BF16)
        along("x", lambda p: logit_own.at[c, p], lambda d: logit_mid.at[k, c, d], first_send.at[1, c], first_recv.at[1, k, c])
        part = jnp.dot(low, w_down[lap, 0], preferred_element_type=F32).reshape(4, 4, TB, RANK)
        for i in range(4):
            proj_own[c, i] = part[i].astype(BF16)
        along("y", lambda p: proj_own.at[c, p], lambda d: proj_mid.at[k, c, d], first_send.at[2, c], first_recv.at[2, k, c])

    def summed(own, arrived):
        total = own.astype(F32)
        for d in range(3):
            total = total + arrived[d].astype(F32)
        return total

    def middle(k, c):
        wait_bytes(square_mid.at[k, c], first_recv.at[0, k, c])
        square_sum[c] = summed(square_own[c], square_mid.at[k, c])
        along("y", lambda p: square_sum.at[c], lambda d: square_in.at[k, c, d], second_send.at[0, c], second_recv.at[0, k, c])
        wait_bytes(logit_mid.at[k, c], first_recv.at[1, k, c])
        logit_sum[c] = summed(logit_own[c, my_x], logit_mid.at[k, c]).astype(BF16)
        along("y", lambda p: logit_sum.at[c, p], lambda d: logit_in.at[k, c, d], second_send.at[1, c], second_recv.at[1, k, c])
        wait_bytes(proj_mid.at[k, c], first_recv.at[2, k, c])
        proj_sum[c] = summed(proj_own[c, my_y], proj_mid.at[k, c]).astype(BF16)
        along("x", lambda p: proj_sum.at[c, p], lambda d: proj_in.at[k, c, d], second_send.at[2, c], second_recv.at[2, k, c])

    def finish(k, c, lap):
        wait_bytes(square_in.at[k, c], second_recv.at[0, k, c])
        total = summed(square_sum[c], square_in.at[k, c])
        at = lax.broadcasted_iota(jnp.int32, (TB, T), 1) == me * TB + lax.broadcasted_iota(jnp.int32, (TB, T), 0)
        own = jnp.sum(jnp.where(at, jnp.broadcast_to(total, (TB, T)), 0.0), axis=1, keepdims=True)
        factor = lax.rsqrt(own / D + EPSILON)

        wait_bytes(logit_in.at[k, c], second_recv.at[1, k, c])
        logits = summed(logit_sum[c, my_y], logit_in.at[k, c])
        gating = jax.nn.sigmoid(logits * factor).astype(BF16)
        mixed = jnp.dot(gating, expert4[lap], preferred_element_type=F32)
        mixed = mixed.astype(BF16).astype(F32)
        lane = lax.broadcasted_iota(jnp.int32, (RP, 128), 1) // EX
        packed = mixed[0:RP]
        for g in range(1, 4):
            packed = jnp.where(lane == g, mixed[g * RP : g * RP + RP], packed)
        mixing[k, c, me] = packed
        to_peers(lambda d, p: mixing.at[k, c, me], lambda d: mixing.at[k, c, me], mixing_send.at[c], mixing_recv.at[k, c])

        wait_bytes(proj_in.at[k, c], second_recv.at[2, k, c])
        projected = summed(proj_sum[c, my_x], proj_in.at[k, c])
        reduced[k, c, me] = (projected * factor).astype(BF16)
        to_peers(lambda d, p: reduced.at[k, c, me], lambda d: reduced.at[k, c, me], reduced_send.at[c], reduced_recv.at[k, c])

    def core_stage(k, c, lap):
        wait_bytes(mixing.at[k, c, pl.ds(0, NT - 1)], mixing_recv.at[k, c])
        packed = mixing[k, c].reshape(NT * RP, 128).astype(BF16)
        weights = jnp.dot(spread[...], packed, preferred_element_type=F32) * group[...]
        weights = jnp.dot(weights.astype(BF16), tile4[...], preferred_element_type=F32)
        wait_bytes(reduced.at[k, c, pl.ds(0, NT - 1)], reduced_recv.at[k, c])
        every = reduced[k, c].astype(F32).reshape(T, RANK).astype(BF16)
        part = lax.dot_general(
            every, w_core[lap, 0].reshape(FB * EX, RANK), NT_DIMS, preferred_element_type=F32
        )
        product = (part * jnp.concatenate([weights] * (FB * EX // 128), axis=1)).astype(BF16)
        ranked_own[k, c] = lax.dot_general(
            selector[...], product, NT_DIMS, preferred_element_type=F32
        ).astype(BF16)
        for d in range(NT):
            pltpu.make_async_remote_copy(
                ranked_own.at[k, c], ranked.at[k, c, me], ranked_send.at[c], ranked_recv.at[k, c],
                device_id={"section": after, "tensor": lax.rem(me + d, NT)}, device_id_type=MESH,
            ).start()

    def advance(k, c, lap):
        wait_bytes(h.at[k + 1, c], h_recv.at[k + 1, c])
        wait_bytes(ranked.at[k, c], ranked_recv.at[k, c])
        update = lax.dot_general(
            ranked[k, c].reshape(RANK, T), up_in[lap, 0], TN_DIMS, preferred_element_type=F32
        )
        h[k + 1, c] = h[k + 1, c] + update

    def hand_on(k, c):
        pltpu.make_async_remote_copy(
            h.at[k, c], h.at[k + 1, c], h_send.at[c], h_recv.at[k + 1, c],
            device_id={"section": after}, device_id_type=MESH,
        ).start()

    def tick(k, carry):
        lap = lap_of(section, k)
        earlier = lap_of(before, k - 1)
        for c in range(C):

            @pl.when(k > 0)
            def _():
                if c == 0:

                    @pl.when(k < 3)
                    def _():
                        which = jnp.where(k == 1, lap_of(before, 0), 1 - lap_of(before, 0))
                        wait_bytes(up_in.at[which], up_recv.at[which])

                advance(k - 1, c, earlier)

            hand_on(k, c)
            project(k, c, lap)

        @pl.when(k == 1)
        def _():
            hand_up(1 - lap_of(section, 0))

        for c in range(C):
            middle(k, c)
        for c in range(C):
            finish(k, c, lap)
        for c in range(C):
            core_stage(k, c, lap)
        return carry

    lax.fori_loop(0, TICKS, tick, 0)
    copies = []
    for c in range(C):
        advance(TICKS - 1, c, lap_of(before, TICKS - 1))
        copies.append(pltpu.make_async_copy(h.at[TICKS, c], out.at[0, pl.ds(c * T, T)], out_sem.at[c]))
        copies[-1].start()
    for c in range(C):
        sums_sent(c)
        wait_bytes(mixing.at[:, c, pl.ds(0, NT - 1)], mixing_send.at[c])
        wait_bytes(reduced.at[:, c, pl.ds(0, NT - 1)], reduced_send.at[c])
        wait_bytes(ranked.at[:, c], ranked_send.at[c])
        wait_bytes(h.at[pl.ds(0, TICKS), c], h_send.at[c])
    for lap in range(2):
        wait_bytes(up_in.at[lap], up_send.at[lap])
    for copy in copies:
        copy.wait()


def per_device(stream, down_factor, router, expert_factor, core_tensor, up_factor):
    operands = (stream, down_factor, router, expert_factor, core_tensor, up_factor)
    dma = pltpu.SemaphoreType.DMA
    return pl.pallas_call(
        kernel,
        out_shape=jax.ShapeDtypeStruct(stream.shape, F32),
        in_specs=[pl.BlockSpec(memory_space=pl.ANY)] * len(operands),
        out_specs=pl.BlockSpec(memory_space=pl.ANY),
        scratch_shapes=[
            pltpu.VMEM(down_factor.shape, BF16),
            pltpu.VMEM(router.shape, BF16),
            pltpu.VMEM(expert_factor.shape, BF16),
            pltpu.VMEM(core_tensor.shape, BF16),
            pltpu.VMEM(up_factor.shape, BF16),
            pltpu.VMEM((2, RANK, 128), BF16),
            pltpu.VMEM((FB, FB * EX), BF16),
            pltpu.VMEM((T, NT * RP), BF16),
            pltpu.VMEM((T, 128), F32),
            pltpu.VMEM((128, 128), BF16),
            pltpu.VMEM((8, MB), BF16),
            pltpu.VMEM((TICKS + 1, C, T, 512), F32),
            pltpu.VMEM((C, 1, T), F32),
            pltpu.VMEM((TICKS, C, 3, 1, T), F32),
            pltpu.VMEM((C, 1, T), F32),
            pltpu.VMEM((TICKS, C, 3, 1, T), F32),
            pltpu.VMEM((C, 4, 4, TB, RANK), BF16),
            pltpu.VMEM((TICKS, C, 3, 4, TB, RANK), BF16),
            pltpu.VMEM((C, 4, TB, RANK), BF16),
            pltpu.VMEM((TICKS, C, 3, TB, RANK), BF16),
            pltpu.VMEM((C, 4, 4, TB, RANK), BF16),
            pltpu.VMEM((TICKS, C, 3, 4, TB, RANK), BF16),
            pltpu.VMEM((C, 4, TB, RANK), BF16),
            pltpu.VMEM((TICKS, C, 3, TB, RANK), BF16),
            pltpu.VMEM((TICKS, C, NT, TB, RANK), BF16),
            pltpu.VMEM((TICKS, C, NT, RP, 128), F32),
            pltpu.VMEM((TICKS, C, FB, T), BF16),
            pltpu.VMEM((TICKS, C, NT, FB, T), BF16),
            dma((C + 4,)),
            dma((2,)),
            dma((2,)),
            dma((C,)),
            dma((TICKS + 1, C)),
            dma((3, C)),
            dma((3, TICKS, C)),
            dma((3, C)),
            dma((3, TICKS, C)),
            dma((C,)),
            dma((TICKS, C)),
            dma((C,)),
            dma((TICKS, C)),
            dma((C,)),
            dma((TICKS, C)),
            dma((C,)),
        ],
        compiler_params=pltpu.CompilerParams(
            collective_id=0, has_side_effects=True, vmem_limit_bytes=60 << 20
        ),
        name="relay_window",
    )(*operands)


def solution(mesh):
    return jax.shard_map(
        per_device,
        mesh=mesh,
        in_specs=(
            P("section", None, "tensor"),
            P(None, "section", "tensor", None),
            P(None, "section", "tensor", None),
            P(None, "section", None, None),
            P(None, "section", "tensor", None, None),
            P(None, "section", None, "tensor"),
        ),
        out_specs=P("section", None, "tensor"),
        check_vma=False,
    )
```

```python
import functools

import jax
import jax.numpy as jnp
from jax import lax
from jax.experimental import pallas as pl
from jax.experimental.pallas import tpu as pltpu
from jax.sharding import PartitionSpec as P

D = 8192
TICKS = 6
EPSILON = 1e-05
MB = 512
RANK = 512
EX = 32
FB = 32
NT = 16
C = 4
T = MB // C
TB = T // NT
RP = TB // 4
MESH = pl.DeviceIdType.MESH
F32 = jnp.float32
BF16 = jnp.bfloat16
NT_DIMS = (((1,), (1,)), ((), ()))
TN_DIMS = (((0,), (0,)), ((), ()))


def kernel(
    stream, down, router, expert, core, up, out,
    w_down, w_router, w_expert, w_core, up_in, expert4, selector, spread, group, tile4, ones,
    h, square_own, square_mid, square_sum, square_in, logit_own, logit_mid, logit_sum, logit_in,
    proj_own, proj_mid, proj_sum, proj_in, reduced, mixing, ranked_own, ranked,
    load_sem, up_send, up_recv, h_send, h_recv, first_send, first_recv, second_send, second_recv, reduced_send, reduced_recv, mixing_send, mixing_recv, ranked_send, ranked_recv, out_sem,
):
    me = lax.axis_index("tensor")
    section = lax.axis_index("section")
    my_y, my_x = me // 4, lax.rem(me, 4)
    sections = lax.axis_size("section")
    after = lax.rem(section + 1, sections)
    before = lax.rem(section + sections - 1, sections)

    loads = []
    for c in range(C):
        loads.append(pltpu.make_async_copy(stream.at[0, pl.ds(c * T, T)], h.at[0, c], load_sem.at[c]))
    for i, (a, b) in enumerate(
        ((router, w_router), (down, w_down), (expert, w_expert), (core, w_core))
    ):
        loads.append(pltpu.make_async_copy(a, b, load_sem.at[C + i]))
    for copy in loads:
        copy.start()

    barrier = pltpu.get_barrier_semaphore()
    for d in range(NT):
        peer = lax.rem(me + d, NT)
        if d:
            pl.semaphore_signal(barrier, inc=1, device_id={"tensor": peer}, device_id_type=MESH)
        pl.semaphore_signal(barrier, inc=1, device_id={"section": before, "tensor": peer}, device_id_type=MESH)

    ones[...] = jnp.ones((8, MB), BF16)
    rows = lax.broadcasted_iota(jnp.int32, (FB, FB * EX), 0)
    columns = lax.broadcasted_iota(jnp.int32, (FB, FB * EX), 1)
    selector[...] = jnp.where(columns // EX == rows, 1.0, 0.0).astype(BF16)
    rows = lax.broadcasted_iota(jnp.int32, (128, 128), 0)
    columns = lax.broadcasted_iota(jnp.int32, (128, 128), 1)
    tile4[...] = jnp.where(rows % EX == columns % EX, 1.0, 0.0).astype(BF16)
    rows = lax.broadcasted_iota(jnp.int32, (T, NT * RP), 0)
    columns = lax.broadcasted_iota(jnp.int32, (T, NT * RP), 1)
    spread[...] = jnp.where((rows // TB == columns // RP) & (rows % RP == columns % RP), 1.0, 0.0).astype(BF16)
    rows = lax.broadcasted_iota(jnp.int32, (T, 128), 0)
    columns = lax.broadcasted_iota(jnp.int32, (T, 128), 1)
    group[...] = jnp.where((rows % TB) // RP == columns // EX, 1.0, 0.0)

    for copy in loads[: C + 2]:
        copy.wait()

    pl.semaphore_wait(barrier, 2 * NT - 1)

    def lap_of(s, k):
        return jnp.where(lax.rem(s - k + sections, sections) < sections // 2, 1, 0) + jnp.where(s < k, 1, 0)

    def hand_up(lap):
        pltpu.make_async_remote_copy(
            up.at[lap], up_in.at[lap], up_send.at[lap], up_recv.at[lap],
            device_id={"section": after}, device_id_type=MESH,
        ).start()

    hand_up(lap_of(section, 0))

    def to_peers(source, target, send, recv):
        for d in range(1, NT):
            peer = lax.rem(me + d, NT)
            pltpu.make_async_remote_copy(
                source(d, peer), target(d), send, recv, device_id={"tensor": peer}, device_id_type=MESH
            ).start()

    def along(axis, source, target, send, recv):
        for d in range(1, 4):
            if axis == "x":
                place = lax.rem(my_x + d, 4)
                peer = my_y * 4 + place
            else:
                place = lax.rem(my_y + d, 4)
                peer = place * 4 + my_x
            pltpu.make_async_remote_copy(
                source(place), target(d - 1), send, recv, device_id={"tensor": peer}, device_id_type=MESH
            ).start()

    def wait_bytes(ref, sem):
        pltpu.make_async_copy(ref, ref, sem).wait()

    def sums_sent(c):
        wait_bytes(square_mid.at[0, c], first_send.at[0, c])
        wait_bytes(logit_mid.at[0, c], first_send.at[1, c])
        wait_bytes(proj_mid.at[0, c], first_send.at[2, c])
        wait_bytes(square_in.at[0, c], second_send.at[0, c])
        wait_bytes(logit_in.at[0, c], second_send.at[1, c])
        wait_bytes(proj_in.at[0, c], second_send.at[2, c])

    def project(k, c, lap):
        x = h[k, c]

        @pl.when(k > 0)
        def _():
            sums_sent(c)

        low = x.astype(BF16)
        part = jnp.dot(low, w_router[lap, 0], preferred_element_type=F32).reshape(4, 4, TB, RANK)
        for i in range(4):
            logit_own[c, i] = part[:, i].astype(BF16)
        along("x", lambda p: logit_own.at[c, p], lambda d: logit_mid.at[k, c, d], first_send.at[1, c], first_recv.at[1, k, c])
        part = jnp.dot(low, w_down[lap, 0], preferred_element_type=F32).reshape(4, 4, TB, RANK)
        for i in range(4):
            proj_own[c, i] = part[i].astype(BF16)
        along("y", lambda p: proj_own.at[c, p], lambda d: proj_mid.at[k, c, d], first_send.at[2, c], first_recv.at[2, k, c])
        squares = lax.dot_general(ones[...], (x * x).astype(BF16), NT_DIMS, preferred_element_type=F32)
        square_own[c] = squares[0:1]
        along("x", lambda p: square_own.at[c], lambda d: square_mid.at[k, c, d], first_send.at[0, c], first_recv.at[0, k, c])

    def summed(own, arrived):
        total = own.astype(F32)
        for d in range(3):
            total = total + arrived[d].astype(F32)
        return total

    def middle(k, c):
        wait_bytes(square_mid.at[k, c], first_recv.at[0, k, c])
        square_sum[c] = summed(square_own[c], square_mid.at[k, c])
        along("y", lambda p: square_sum.at[c], lambda d: square_in.at[k, c, d], second_send.at[0, c], second_recv.at[0, k, c])
        wait_bytes(logit_mid.at[k, c], first_recv.at[1, k, c])
        logit_sum[c] = summed(logit_own[c, my_x], logit_mid.at[k, c]).astype(BF16)
        along("y", lambda p: logit_sum.at[c, p], lambda d: logit_in.at[k, c, d], second_send.at[1, c], second_recv.at[1, k, c])
        wait_bytes(proj_mid.at[k, c], first_recv.at[2, k, c])
        proj_sum[c] = summed(proj_own[c, my_y], proj_mid.at[k, c]).astype(BF16)
        along("x", lambda p: proj_sum.at[c, p], lambda d: proj_in.at[k, c, d], second_send.at[2, c], second_recv.at[2, k, c])

    def finish(k, c, lap):
        wait_bytes(proj_in.at[k, c], second_recv.at[2, k, c])
        projected = summed(proj_sum[c, my_x], proj_in.at[k, c])
        reduced[k, c, me] = projected.astype(BF16)
        to_peers(lambda d, p: reduced.at[k, c, me], lambda d: reduced.at[k, c, me], reduced_send.at[c], reduced_recv.at[k, c])
        wait_bytes(square_in.at[k, c], second_recv.at[0, k, c])
        total = summed(square_sum[c], square_in.at[k, c])
        at = lax.broadcasted_iota(jnp.int32, (TB, T), 1) == me * TB + lax.broadcasted_iota(jnp.int32, (TB, T), 0)
        own = jnp.sum(jnp.where(at, jnp.broadcast_to(total, (TB, T)), 0.0), axis=1, keepdims=True)
        factor = lax.rsqrt(own / D + EPSILON)

        wait_bytes(logit_in.at[k, c], second_recv.at[1, k, c])
        logits = summed(logit_sum[c, my_y], logit_in.at[k, c])
        gating = jax.nn.sigmoid(logits * factor).astype(BF16)
        mixed = lax.dot_general(gating, expert4[lap], NT_DIMS, preferred_element_type=F32) * factor
        lane = lax.broadcasted_iota(jnp.int32, (RP, 128), 1) // EX
        packed = mixed[0:RP]
        for g in range(1, 4):
            packed = jnp.where(lane == g, mixed[g * RP : g * RP + RP], packed)
        mixing[k, c, me] = packed.astype(BF16)
        to_peers(lambda d, p: mixing.at[k, c, me], lambda d: mixing.at[k, c, me], mixing_send.at[c], mixing_recv.at[k, c])

    def core_stage(k, c, lap):
        wait_bytes(reduced.at[k, c, pl.ds(0, NT - 1)], reduced_recv.at[k, c])
        every = reduced[k, c].astype(F32).reshape(T, RANK).astype(BF16)
        part = lax.dot_general(
            every, w_core[lap, 0].reshape(FB * EX, RANK), NT_DIMS, preferred_element_type=F32
        )
        wait_bytes(mixing.at[k, c, pl.ds(0, NT - 1)], mixing_recv.at[k, c])
        packed = mixing[k, c].astype(F32).reshape(NT * RP, 128).astype(BF16)
        weights = jnp.dot(spread[...], packed, preferred_element_type=F32) * group[...]
        weights = jnp.dot(weights.astype(BF16), tile4[...], preferred_element_type=F32)
        product = (part * jnp.concatenate([weights] * (FB * EX // 128), axis=1)).astype(BF16)
        ranked_own[k, c] = lax.dot_general(
            selector[...], product, NT_DIMS, preferred_element_type=F32
        ).astype(BF16)
        for d in range(NT):
            pltpu.make_async_remote_copy(
                ranked_own.at[k, c], ranked.at[k, c, me], ranked_send.at[c], ranked_recv.at[k, c],
                device_id={"section": after, "tensor": lax.rem(me + d, NT)}, device_id_type=MESH,
            ).start()

    def advance(k, c, lap):
        wait_bytes(h.at[k + 1, c], h_recv.at[k + 1, c])
        wait_bytes(ranked.at[k, c], ranked_recv.at[k, c])
        update = lax.dot_general(
            ranked[k, c].reshape(RANK, T), up_in[lap, 0], TN_DIMS, preferred_element_type=F32
        )
        h[k + 1, c] = h[k + 1, c] + update

    def hand_on(k, c):
        pltpu.make_async_remote_copy(
            h.at[k, c], h.at[k + 1, c], h_send.at[c], h_recv.at[k + 1, c],
            device_id={"section": after}, device_id_type=MESH,
        ).start()

    def tick(k, carry):
        lap = lap_of(section, k)
        earlier = lap_of(before, k - 1)
        for c in range(C):

            @pl.when(k > 0)
            def _():
                if c == 0:

                    @pl.when(k < 3)
                    def _():
                        which = jnp.where(k == 1, lap_of(before, 0), 1 - lap_of(before, 0))
                        wait_bytes(up_in.at[which], up_recv.at[which])

                advance(k - 1, c, earlier)

            project(k, c, lap)
            hand_on(k, c)

        @pl.when(k == 1)
        def _():
            hand_up(1 - lap_of(section, 0))

        for c in range(C):
            middle(k, c)
        @pl.when(k == 0)
        def _():
            loads[C + 2].wait()
            for i in range(2):
                one = w_expert[i, 0]
                expert4[i] = jnp.concatenate([one, one, one, one], axis=0)

        for c in range(C):
            finish(k, c, lap)

        @pl.when(k == 0)
        def _():
            loads[C + 3].wait()

        for c in range(C):
            core_stage(k, c, lap)
        return carry

    lax.fori_loop(0, TICKS, tick, 0)
    copies = []
    for c in range(C):
        advance(TICKS - 1, c, lap_of(before, TICKS - 1))
        copies.append(pltpu.make_async_copy(h.at[TICKS, c], out.at[0, pl.ds(c * T, T)], out_sem.at[c]))
        copies[-1].start()
    for c in range(C):
        sums_sent(c)
        wait_bytes(mixing.at[:, c, pl.ds(0, NT - 1)], mixing_send.at[c])
        wait_bytes(reduced.at[:, c, pl.ds(0, NT - 1)], reduced_send.at[c])
        wait_bytes(ranked.at[:, c], ranked_send.at[c])
        wait_bytes(h.at[pl.ds(0, TICKS), c], h_send.at[c])
    for lap in range(2):
        wait_bytes(up_in.at[lap], up_send.at[lap])
    for copy in copies:
        copy.wait()


def per_device(stream, down_factor, router, expert_factor, core_tensor, up_factor):
    expert_factor = jnp.swapaxes(expert_factor, 2, 3)
    operands = (stream, down_factor, router, expert_factor, core_tensor, up_factor)
    dma = pltpu.SemaphoreType.DMA
    return pl.pallas_call(
        kernel,
        out_shape=jax.ShapeDtypeStruct(stream.shape, F32),
        in_specs=[pl.BlockSpec(memory_space=pl.ANY)] * len(operands),
        out_specs=pl.BlockSpec(memory_space=pl.ANY),
        scratch_shapes=[
            pltpu.VMEM(down_factor.shape, BF16),
            pltpu.VMEM(router.shape, BF16),
            pltpu.VMEM(expert_factor.shape, BF16),
            pltpu.VMEM(core_tensor.shape, BF16),
            pltpu.VMEM(up_factor.shape, BF16),
            pltpu.VMEM((2, 128, RANK), BF16),
            pltpu.VMEM((FB, FB * EX), BF16),
            pltpu.VMEM((T, NT * RP), BF16),
            pltpu.VMEM((T, 128), F32),
            pltpu.VMEM((128, 128), BF16),
            pltpu.VMEM((8, MB), BF16),
            pltpu.VMEM((TICKS + 1, C, T, 512), F32),
            pltpu.VMEM((C, 1, T), F32),
            pltpu.VMEM((TICKS, C, 3, 1, T), F32),
            pltpu.VMEM((C, 1, T), F32),
            pltpu.VMEM((TICKS, C, 3, 1, T), F32),
            pltpu.VMEM((C, 4, 4, TB, RANK), BF16),
            pltpu.VMEM((TICKS, C, 3, 4, TB, RANK), BF16),
            pltpu.VMEM((C, 4, TB, RANK), BF16),
            pltpu.VMEM((TICKS, C, 3, TB, RANK), BF16),
            pltpu.VMEM((C, 4, 4, TB, RANK), BF16),
            pltpu.VMEM((TICKS, C, 3, 4, TB, RANK), BF16),
            pltpu.VMEM((C, 4, TB, RANK), BF16),
            pltpu.VMEM((TICKS, C, 3, TB, RANK), BF16),
            pltpu.VMEM((TICKS, C, NT, TB, RANK), BF16),
            pltpu.VMEM((TICKS, C, NT, RP, 128), BF16),
            pltpu.VMEM((TICKS, C, FB, T), BF16),
            pltpu.VMEM((TICKS, C, NT, FB, T), BF16),
            dma((C + 4,)),
            dma((2,)),
            dma((2,)),
            dma((C,)),
            dma((TICKS + 1, C)),
            dma((3, C)),
            dma((3, TICKS, C)),
            dma((3, C)),
            dma((3, TICKS, C)),
            dma((C,)),
            dma((TICKS, C)),
            dma((C,)),
            dma((TICKS, C)),
            dma((C,)),
            dma((TICKS, C)),
            dma((C,)),
        ],
        compiler_params=pltpu.CompilerParams(
            collective_id=0, has_side_effects=True, vmem_limit_bytes=60 << 20
        ),
        name="relay_window",
    )(*operands)


def solution(mesh):
    return jax.shard_map(
        per_device,
        mesh=mesh,
        in_specs=(
            P("section", None, "tensor"),
            P(None, "section", "tensor", None),
            P(None, "section", "tensor", None),
            P(None, "section", None, None),
            P(None, "section", "tensor", None, None),
            P(None, "section", None, "tensor"),
        ),
        out_specs=P("section", None, "tensor"),
        check_vma=False,
    )
```

```python
import functools

import jax
import jax.numpy as jnp
from jax import lax
from jax.experimental import pallas as pl
from jax.experimental.pallas import tpu as pltpu
from jax.sharding import PartitionSpec as P

D = 8192
TICKS = 6
EPSILON = 1e-05
MB = 512
RANK = 512
EX = 32
FB = 32
NT = 16
C = 4
T = MB // C
TB = T // NT
RP = TB // 4
FAR_FIRST = sorted(
    ((dy, dx) for dy in range(4) for dx in range(4)), key=lambda o: -sum(min(v, 4 - v) for v in o)
)
MESH = pl.DeviceIdType.MESH
F32 = jnp.float32
BF16 = jnp.bfloat16
NT_DIMS = (((1,), (1,)), ((), ()))
TN_DIMS = (((0,), (0,)), ((), ()))


def kernel(
    stream, down, router, expert, core, up, out,
    w_down, w_router, w_expert, w_core, up_in, expert4, selector, spread, group, tile4, ones,
    h, square_own, square_mid, square_sum, square_in, logit_own, logit_mid, logit_sum, logit_in,
    proj_own, proj_mid, proj_sum, proj_in, reduced, mixing, ranked_own, ranked,
    load_sem, up_send, up_recv, h_send, h_recv, first_send, first_recv, second_send, second_recv, reduced_send, reduced_recv, mixing_send, mixing_recv, ranked_send, ranked_recv, out_sem,
):
    me = lax.axis_index("tensor")
    section = lax.axis_index("section")
    my_y, my_x = me // 4, lax.rem(me, 4)
    sections = lax.axis_size("section")
    after = lax.rem(section + 1, sections)
    before = lax.rem(section + sections - 1, sections)

    loads = []
    for c in range(C):
        loads.append(pltpu.make_async_copy(stream.at[0, pl.ds(c * T, T)], h.at[0, c], load_sem.at[c]))
    for i, (a, b) in enumerate(
        ((router, w_router), (down, w_down), (expert, w_expert), (core, w_core))
    ):
        loads.append(pltpu.make_async_copy(a, b, load_sem.at[C + i]))
    for copy in loads:
        copy.start()

    barrier = pltpu.get_barrier_semaphore()
    for d in range(NT):
        peer = lax.rem(me + d, NT)
        if d:
            pl.semaphore_signal(barrier, inc=1, device_id={"tensor": peer}, device_id_type=MESH)
        pl.semaphore_signal(barrier, inc=1, device_id={"section": before, "tensor": peer}, device_id_type=MESH)

    ones[...] = jnp.ones((8, MB), BF16)
    rows = lax.broadcasted_iota(jnp.int32, (FB, FB * EX), 0)
    columns = lax.broadcasted_iota(jnp.int32, (FB, FB * EX), 1)
    selector[...] = jnp.where(columns // EX == rows, 1.0, 0.0).astype(BF16)
    rows = lax.broadcasted_iota(jnp.int32, (128, 128), 0)
    columns = lax.broadcasted_iota(jnp.int32, (128, 128), 1)
    tile4[...] = jnp.where(rows % EX == columns % EX, 1.0, 0.0).astype(BF16)
    rows = lax.broadcasted_iota(jnp.int32, (T, NT * RP), 0)
    columns = lax.broadcasted_iota(jnp.int32, (T, NT * RP), 1)
    spread[...] = jnp.where((rows // TB == columns // RP) & (rows % RP == columns % RP), 1.0, 0.0).astype(BF16)
    rows = lax.broadcasted_iota(jnp.int32, (T, 128), 0)
    columns = lax.broadcasted_iota(jnp.int32, (T, 128), 1)
    group[...] = jnp.where((rows % TB) // RP == columns // EX, 1.0, 0.0)

    for copy in loads[: C + 2]:
        copy.wait()

    pl.semaphore_wait(barrier, 2 * NT - 1)

    def lap_of(s, k):
        return jnp.where(lax.rem(s - k + sections, sections) < sections // 2, 1, 0) + jnp.where(s < k, 1, 0)

    def hand_up(lap):
        pltpu.make_async_remote_copy(
            up.at[lap], up_in.at[lap], up_send.at[lap], up_recv.at[lap],
            device_id={"section": after}, device_id_type=MESH,
        ).start()

    hand_up(lap_of(section, 0))

    def to_peers(source, target, send, recv):
        for dy, dx in FAR_FIRST[:-1]:
            peer = lax.rem(my_y + dy, 4) * 4 + lax.rem(my_x + dx, 4)
            pltpu.make_async_remote_copy(
                source(peer), target(), send, recv, device_id={"tensor": peer}, device_id_type=MESH
            ).start()

    def along(axis, source, target, send, recv):
        for d in (2, 1, 3):
            if axis == "x":
                place = lax.rem(my_x + d, 4)
                peer = my_y * 4 + place
            else:
                place = lax.rem(my_y + d, 4)
                peer = place * 4 + my_x
            pltpu.make_async_remote_copy(
                source(place), target(d - 1), send, recv, device_id={"tensor": peer}, device_id_type=MESH
            ).start()

    def wait_bytes(ref, sem):
        pltpu.make_async_copy(ref, ref, sem).wait()

    def sums_sent(c):
        wait_bytes(square_mid.at[0, c], first_send.at[0, c])
        wait_bytes(logit_mid.at[0, c], first_send.at[1, c])
        wait_bytes(proj_mid.at[0, c], first_send.at[2, c])
        wait_bytes(square_in.at[0, c], second_send.at[0, c])
        wait_bytes(logit_in.at[0, c], second_send.at[1, c])
        wait_bytes(proj_in.at[0, c], second_send.at[2, c])

    def project(k, c, lap):
        x = h[k, c]

        @pl.when(k > 0)
        def _():
            sums_sent(c)

        low = x.astype(BF16)
        part = jnp.dot(low, w_router[lap, 0], preferred_element_type=F32).reshape(4, 4, TB, RANK)
        for i in range(4):
            logit_own[c, i] = part[:, i].astype(BF16)
        along("x", lambda p: logit_own.at[c, p], lambda d: logit_mid.at[k, c, d], first_send.at[1, c], first_recv.at[1, k, c])
        part = jnp.dot(low, w_down[lap, 0], preferred_element_type=F32).reshape(4, 4, TB, RANK)
        for i in range(4):
            proj_own[c, i] = part[i].astype(BF16)
        along("y", lambda p: proj_own.at[c, p], lambda d: proj_mid.at[k, c, d], first_send.at[2, c], first_recv.at[2, k, c])
        squares = lax.dot_general(ones[...], (x * x).astype(BF16), NT_DIMS, preferred_element_type=F32)
        square_own[c] = squares[0:1]
        along("x", lambda p: square_own.at[c], lambda d: square_mid.at[k, c, d], first_send.at[0, c], first_recv.at[0, k, c])

    def summed(own, arrived):
        total = own.astype(F32)
        for d in range(3):
            total = total + arrived[d].astype(F32)
        return total

    def middle(k, c):
        wait_bytes(square_mid.at[k, c], first_recv.at[0, k, c])
        square_sum[c] = summed(square_own[c], square_mid.at[k, c])
        along("y", lambda p: square_sum.at[c], lambda d: square_in.at[k, c, d], second_send.at[0, c], second_recv.at[0, k, c])
        wait_bytes(logit_mid.at[k, c], first_recv.at[1, k, c])
        logit_sum[c] = summed(logit_own[c, my_x], logit_mid.at[k, c]).astype(BF16)
        along("y", lambda p: logit_sum.at[c, p], lambda d: logit_in.at[k, c, d], second_send.at[1, c], second_recv.at[1, k, c])
        wait_bytes(proj_mid.at[k, c], first_recv.at[2, k, c])
        proj_sum[c] = summed(proj_own[c, my_y], proj_mid.at[k, c]).astype(BF16)
        along("x", lambda p: proj_sum.at[c, p], lambda d: proj_in.at[k, c, d], second_send.at[2, c], second_recv.at[2, k, c])

    def finish(k, c, lap):
        wait_bytes(proj_in.at[k, c], second_recv.at[2, k, c])
        projected = summed(proj_sum[c, my_x], proj_in.at[k, c])
        reduced[k, c, me] = projected.astype(BF16)
        to_peers(lambda p: reduced.at[k, c, me], lambda: reduced.at[k, c, me], reduced_send.at[c], reduced_recv.at[k, c])
        wait_bytes(square_in.at[k, c], second_recv.at[0, k, c])
        total = summed(square_sum[c], square_in.at[k, c])
        at = lax.broadcasted_iota(jnp.int32, (TB, T), 1) == me * TB + lax.broadcasted_iota(jnp.int32, (TB, T), 0)
        own = jnp.sum(jnp.where(at, jnp.broadcast_to(total, (TB, T)), 0.0), axis=1, keepdims=True)
        factor = lax.rsqrt(own / D + EPSILON)

        wait_bytes(logit_in.at[k, c], second_recv.at[1, k, c])
        logits = summed(logit_sum[c, my_y], logit_in.at[k, c])
        gating = jax.nn.sigmoid(logits * factor).astype(BF16)
        mixed = lax.dot_general(gating, expert4[lap], NT_DIMS, preferred_element_type=F32) * factor
        lane = lax.broadcasted_iota(jnp.int32, (RP, 128), 1) // EX
        packed = mixed[0:RP]
        for g in range(1, 4):
            packed = jnp.where(lane == g, mixed[g * RP : g * RP + RP], packed)
        mixing[k, c, me] = packed.astype(BF16)
        to_peers(lambda p: mixing.at[k, c, me], lambda: mixing.at[k, c, me], mixing_send.at[c], mixing_recv.at[k, c])

    def core_stage(k, c, lap):
        wait_bytes(reduced.at[k, c, pl.ds(0, NT - 1)], reduced_recv.at[k, c])
        every = reduced[k, c].astype(F32).reshape(T, RANK).astype(BF16)
        part = lax.dot_general(
            every, w_core[lap, 0].reshape(FB * EX, RANK), NT_DIMS, preferred_element_type=F32
        )
        wait_bytes(mixing.at[k, c, pl.ds(0, NT - 1)], mixing_recv.at[k, c])
        packed = mixing[k, c].astype(F32).reshape(NT * RP, 128).astype(BF16)
        weights = jnp.dot(spread[...], packed, preferred_element_type=F32) * group[...]
        weights = jnp.dot(weights.astype(BF16), tile4[...], preferred_element_type=F32)
        product = (part * jnp.concatenate([weights] * (FB * EX // 128), axis=1)).astype(BF16)
        ranked_own[k, c] = lax.dot_general(
            selector[...], product, NT_DIMS, preferred_element_type=F32
        ).astype(BF16)
        for dy, dx in FAR_FIRST:
            peer = lax.rem(my_y + dy, 4) * 4 + lax.rem(my_x + dx, 4)
            pltpu.make_async_remote_copy(
                ranked_own.at[k, c], ranked.at[k, c, me], ranked_send.at[c], ranked_recv.at[k, c],
                device_id={"section": after, "tensor": peer}, device_id_type=MESH,
            ).start()

    def advance(k, c, lap):
        wait_bytes(h.at[k + 1, c], h_recv.at[k + 1, c])
        wait_bytes(ranked.at[k, c], ranked_recv.at[k, c])
        update = lax.dot_general(
            ranked[k, c].reshape(RANK, T), up_in[lap, 0], TN_DIMS, preferred_element_type=F32
        )
        h[k + 1, c] = h[k + 1, c] + update

    def hand_on(k, c):
        pltpu.make_async_remote_copy(
            h.at[k, c], h.at[k + 1, c], h_send.at[c], h_recv.at[k + 1, c],
            device_id={"section": after}, device_id_type=MESH,
        ).start()

    def tick(k, carry):
        lap = lap_of(section, k)
        earlier = lap_of(before, k - 1)
        for c in range(C):

            @pl.when(k > 0)
            def _():
                if c == 0:

                    @pl.when(k < 3)
                    def _():
                        which = jnp.where(k == 1, lap_of(before, 0), 1 - lap_of(before, 0))
                        wait_bytes(up_in.at[which], up_recv.at[which])

                advance(k - 1, c, earlier)

            project(k, c, lap)
            hand_on(k, c)

        @pl.when(k == 1)
        def _():
            hand_up(1 - lap_of(section, 0))

        for c in range(C):
            middle(k, c)
        @pl.when(k == 0)
        def _():
            loads[C + 2].wait()
            for i in range(2):
                one = w_expert[i, 0]
                expert4[i] = jnp.concatenate([one, one, one, one], axis=0)

        for c in range(C):
            finish(k, c, lap)

        @pl.when(k == 0)
        def _():
            loads[C + 3].wait()

        for c in range(C):
            core_stage(k, c, lap)
        return carry

    lax.fori_loop(0, TICKS, tick, 0)
    copies = []
    for c in range(C):
        advance(TICKS - 1, c, lap_of(before, TICKS - 1))
        copies.append(pltpu.make_async_copy(h.at[TICKS, c], out.at[0, pl.ds(c * T, T)], out_sem.at[c]))
        copies[-1].start()
    for c in range(C):
        sums_sent(c)
        wait_bytes(mixing.at[:, c, pl.ds(0, NT - 1)], mixing_send.at[c])
        wait_bytes(reduced.at[:, c, pl.ds(0, NT - 1)], reduced_send.at[c])
        wait_bytes(ranked.at[:, c], ranked_send.at[c])
        wait_bytes(h.at[pl.ds(0, TICKS), c], h_send.at[c])
    for lap in range(2):
        wait_bytes(up_in.at[lap], up_send.at[lap])
    for copy in copies:
        copy.wait()


def per_device(stream, down_factor, router, expert_factor, core_tensor, up_factor):
    expert_factor = jnp.swapaxes(expert_factor, 2, 3)
    operands = (stream, down_factor, router, expert_factor, core_tensor, up_factor)
    dma = pltpu.SemaphoreType.DMA
    return pl.pallas_call(
        kernel,
        out_shape=jax.ShapeDtypeStruct(stream.shape, F32),
        in_specs=[pl.BlockSpec(memory_space=pl.ANY)] * len(operands),
        out_specs=pl.BlockSpec(memory_space=pl.ANY),
        scratch_shapes=[
            pltpu.VMEM(down_factor.shape, BF16),
            pltpu.VMEM(router.shape, BF16),
            pltpu.VMEM(expert_factor.shape, BF16),
            pltpu.VMEM(core_tensor.shape, BF16),
            pltpu.VMEM(up_factor.shape, BF16),
            pltpu.VMEM((2, 128, RANK), BF16),
            pltpu.VMEM((FB, FB * EX), BF16),
            pltpu.VMEM((T, NT * RP), BF16),
            pltpu.VMEM((T, 128), F32),
            pltpu.VMEM((128, 128), BF16),
            pltpu.VMEM((8, MB), BF16),
            pltpu.VMEM((TICKS + 1, C, T, 512), F32),
            pltpu.VMEM((C, 1, T), F32),
            pltpu.VMEM((TICKS, C, 3, 1, T), F32),
            pltpu.VMEM((C, 1, T), F32),
            pltpu.VMEM((TICKS, C, 3, 1, T), F32),
            pltpu.VMEM((C, 4, 4, TB, RANK), BF16),
            pltpu.VMEM((TICKS, C, 3, 4, TB, RANK), BF16),
            pltpu.VMEM((C, 4, TB, RANK), BF16),
            pltpu.VMEM((TICKS, C, 3, TB, RANK), BF16),
            pltpu.VMEM((C, 4, 4, TB, RANK), BF16),
            pltpu.VMEM((TICKS, C, 3, 4, TB, RANK), BF16),
            pltpu.VMEM((C, 4, TB, RANK), BF16),
            pltpu.VMEM((TICKS, C, 3, TB, RANK), BF16),
            pltpu.VMEM((TICKS, C, NT, TB, RANK), BF16),
            pltpu.VMEM((TICKS, C, NT, RP, 128), BF16),
            pltpu.VMEM((TICKS, C, FB, T), BF16),
            pltpu.VMEM((TICKS, C, NT, FB, T), BF16),
            dma((C + 4,)),
            dma((2,)),
            dma((2,)),
            dma((C,)),
            dma((TICKS + 1, C)),
            dma((3, C)),
            dma((3, TICKS, C)),
            dma((3, C)),
            dma((3, TICKS, C)),
            dma((C,)),
            dma((TICKS, C)),
            dma((C,)),
            dma((TICKS, C)),
            dma((C,)),
            dma((TICKS, C)),
            dma((C,)),
        ],
        compiler_params=pltpu.CompilerParams(
            collective_id=0, has_side_effects=True, vmem_limit_bytes=60 << 20
        ),
        name="relay_window",
    )(*operands)


def solution(mesh):
    return jax.shard_map(
        per_device,
        mesh=mesh,
        in_specs=(
            P("section", None, "tensor"),
            P(None, "section", "tensor", None),
            P(None, "section", "tensor", None),
            P(None, "section", None, None),
            P(None, "section", "tensor", None, None),
            P(None, "section", None, "tensor"),
        ),
        out_specs=P("section", None, "tensor"),
        check_vma=False,
    )
```
